256 devices in a mesh: dom: 32 (over z, y), batch: 8 (over x, core).
Axes of the slice: x: 4, y: 4, z: 8, core: 2. Of those that a mesh axis runs over, the one named last changes fastest.
Arguments:
- activations: bfloat16 [2048, 65536], P('batch', 'dom'), may hold values from 0 to 2
- tile_weights: bfloat16 [4, 512, 512, 128], P(None, 'dom', 'batch'), may hold values from -0.375 to 0.375
- biases: float32 [4, 65536], P(None, 'dom'), may hold values from -2.5 to 2.5
- source_codes: int32 [4, 512, 4], P(None, 'dom'), may hold values from 0 to 19
- send_list: int32 [4, 32, 4], P(None, 'dom'), may hold values from 0 to 15
Outputs:
- result: bfloat16 [2048, 65536], P('batch', 'dom')
The draws below stay inside these ranges and needn't reach their ends.
All inputs are finite; a program needn't handle non-finite values.
Results may differ from the reference program's by a relative error of at most 0.0062.
Values may be sent and summed in bfloat16 or wider, within the bound.
A program may use at most 64 MiB of HBM per device.

```python
import jax
import jax.numpy as jnp
from jax import lax

NEURONS = 65536
TILE = 128
FANIN = 4
NEIGH = 4
LAYERS = 4
ROWS = 2048
BLOCKS = 512
BLK_DEV = 16
PARTS_SIZE = 32


def plant(values, key, low, top_value):
    place = [jax.random.randint(jax.random.fold_in(key, axis), (), 0, length) for axis, length in enumerate(values.shape)]
    main_axis = values.shape.index(max(values.shape))
    beside = place[:main_axis] + [(place[main_axis] + 1) % values.shape[main_axis]] + place[main_axis + 1:]
    return values.at[tuple(place)].set(low).at[tuple(beside)].set(top_value)


def steps_of(rng, shape, shards, low, top_value):
    def one(dim, blocks):
        heights = jax.random.uniform(jax.random.fold_in(jax.random.fold_in(rng, 6), dim), (blocks,), jnp.float32, low / len(shards), top_value / len(shards))
        return jnp.repeat(jnp.exp(heights), shape[dim] // blocks).reshape((-1,) + (1,) * (len(shape) - dim - 1))

    factor_of = one(*shards[0])
    for cut in shards[1:]:
        factor_of = factor_of * one(*cut)
    return factor_of


def centred(rng, dims, spread, bound, cuts=(), dtype=jnp.bfloat16):
    factor_of = steps_of(rng, dims, cuts, -0.22, 0.18) if cuts else 1.0
    result = jax.random.normal(rng, dims, jnp.float32) * spread * factor_of
    return jnp.minimum(jnp.maximum(result, -bound), bound).astype(dtype)


def setup_inputs(seed: int = 0) -> dict:
    streams_of = jax.random.split(jax.random.key(seed), 6)
    activations = jnp.clip(2.0 * jax.random.uniform(streams_of[0], (ROWS, NEURONS), jnp.float32) ** steps_of(streams_of[0], (ROWS, NEURONS), ((0, 8), (1, 32)), -0.2, 0.2), 0.0, 2.0).astype(jnp.bfloat16)
    tile_weights = centred(streams_of[1], (LAYERS, BLOCKS, FANIN * TILE, TILE), (FANIN * TILE // 2) ** -0.5, 0.375, ((1, 32), (2, 8)))
    biases = centred(streams_of[2], (LAYERS, NEURONS), 0.5, 2.5, ((1, 32),), jnp.float32)
    source_codes = plant(jax.random.randint(streams_of[3], (LAYERS, BLOCKS, FANIN), 0, BLK_DEV + NEIGH), jax.random.fold_in(streams_of[3], 1), 0, (BLK_DEV + NEIGH) - 1).astype(jnp.int32)
    send_list = plant(jax.random.randint(streams_of[4], (LAYERS, PARTS_SIZE, NEIGH), 0, BLK_DEV), jax.random.fold_in(streams_of[4], 1), 0, BLK_DEV - 1).astype(jnp.int32)
    return dict(activations=activations, tile_weights=tile_weights, biases=biases, source_codes=source_codes, send_list=send_list)


def source_blocks(code_table, send_table):
    partition = (jnp.arange(BLOCKS) // BLK_DEV).astype(jnp.int32)[:, None]
    offset_table = jnp.array((1, 2, -1, PARTS_SIZE // 2), jnp.int32)
    slot_index = jnp.clip(code_table - BLK_DEV, 0, NEIGH - 1).astype(jnp.int32)
    sender_part = ((partition - offset_table[slot_index]) % PARTS_SIZE).astype(jnp.int32)
    remote_block = sender_part * BLK_DEV + send_table[sender_part, slot_index]
    local_block = partition * BLK_DEV + code_table
    return jnp.where(code_table < BLK_DEV, local_block, remote_block).astype(jnp.int32)


def reference(activations, tile_weights, biases, source_codes, send_list):
    current = activations
    group_count = BLOCKS // 16
    for layer_index in range(LAYERS):
        sources = source_blocks(source_codes[layer_index], send_list[layer_index])
        blocked = current.reshape(ROWS, BLOCKS, TILE)
        group_sources = sources.reshape(group_count, 16 * FANIN)
        group_tiles = tile_weights[layer_index].reshape(group_count, 16, FANIN * TILE, TILE)
        group_bias = biases[layer_index].reshape(group_count, 16, TILE)

        def one_group(pieces):
            index_row, weight_group, bias_group = pieces
            input_panel = jnp.take(blocked, index_row, axis=1).reshape(ROWS, 16, FANIN * TILE)
            summed = jnp.einsum("rjc,jco->rjo", input_panel.astype(jnp.float32), weight_group.astype(jnp.float32))
            return summed + bias_group[None].astype(jnp.float32)

        outputs = lax.map(one_group, (group_sources, group_tiles, group_bias))
        outputs = jnp.transpose(outputs, (1, 0, 2, 3)).reshape(ROWS, NEURONS)
        current = jnp.maximum(outputs, 0.0).astype(jnp.bfloat16)
    return current
```

```python
import jax
import jax.numpy as jnp
from jax import lax
from jax.experimental import pallas as pl
from jax.experimental.pallas import tpu as pltpu
from jax.sharding import PartitionSpec as P

MESH = pl.DeviceIdType.MESH
LAYERS, BLK, FAN, TILE, NEIGH = 4, 16, 4, 128, 4
CHIPS, CORES = 4, 2
SHARDS = CHIPS * CORES
HALF = BLK // 2


def kernel(parts, rows, act, weights, biases, codes, sends, out, *scratch):
    wbufs, pools, stages = scratch[0:4], scratch[4:8], scratch[8:12]
    first, final, bias_v = scratch[12:15]
    xs_send, xs_recv, pt_send, pt_recv, bd_send, bd_recv, ld_sem, out_sem = scratch[15:]

    dom = lax.axis_index("dom")
    me = lax.axis_index("batch")
    chip, core = me // CORES, me % CORES
    right = lax.rem(chip + 1, CHIPS) * CORES + core
    left = lax.rem(chip + CHIPS - 1, CHIPS) * CORES + core
    far = lax.rem(chip + 2, CHIPS) * CORES + core
    partner = chip * CORES + 1 - core
    offsets = (1, 2, parts - 1, parts // 2)

    loads = []

    def load(source, target):
        copy = pltpu.make_async_copy(source, target, ld_sem.at[len(loads)])
        copy.start()
        loads.append(copy)

    load(weights.at[0], wbufs[0].at[me])
    for j in range(BLK):
        load(act.at[:, pl.ds(j * TILE, TILE)], first.at[j])
    for l in range(1, LAYERS):
        load(weights.at[l], wbufs[l].at[me])
    for j in range(BLK):
        load(biases.at[:, pl.ds(j * TILE, TILE)], bias_v.at[j])
    for j in range(BLK):
        load(act.at[:, pl.ds(j * TILE, TILE)], pools[0].at[j])

    barrier = pltpu.get_barrier_semaphore()
    for peer in (left, right, partner):
        pl.semaphore_signal(barrier, inc=1, device_id={"batch": peer}, device_id_type=MESH)
    for offset in offsets:
        sender = lax.rem(dom + parts - offset, parts)
        pl.semaphore_signal(barrier, inc=1, device_id={"dom": sender}, device_id_type=MESH)
    pl.semaphore_wait(barrier, 7)

    started = []

    def piece(l, b, h):
        return wbufs[l].at[b, pl.ds(h * HALF, HALF)]

    def ring(l, direction, slot, b):
        half = (direction if slot != 1 else 1 - direction)
        ref = piece(l, b, half)
        return pltpu.make_async_remote_copy(
            src_ref=ref, dst_ref=ref,
            send_sem=xs_send.at[l, direction, slot], recv_sem=xs_recv.at[l, direction, slot],
            device_id={"batch": right if direction == 0 else left}, device_id_type=MESH)

    def ring_start(l, direction, slot, b):
        copy = ring(l, direction, slot, b)
        copy.start()
        started.append(copy)

    origin = ((left, left, far), (right, right, far))

    def ring_wait(l, direction, slot):
        ring(l, direction, slot, origin[direction][slot]).wait_recv()

    def hand(l, slot, ref):
        return pltpu.make_async_remote_copy(
            src_ref=ref, dst_ref=ref, send_sem=pt_send.at[l, slot], recv_sem=pt_recv.at[l, slot],
            device_id={"batch": partner}, device_id_type=MESH)

    def hand_start(l, slot, ref):
        copy = hand(l, slot, ref)
        copy.start()
        started.append(copy)

    def hand_wait(l):
        for slot in range(6):
            direction, s = slot % 2, slot // 2
            half = (direction if s != 1 else 1 - direction)
            b = origin[direction][s] + 1 - 2 * core
            hand(l, slot, piece(l, b, half)).wait_recv()
        hand(l, 6, wbufs[l].at[partner]).wait_recv()

    def boundary(l, i):
        return pltpu.make_async_remote_copy(
            src_ref=stages[l].at[i], dst_ref=pools[l].at[BLK + i],
            send_sem=bd_send.at[l, i], recv_sem=bd_recv.at[l, i],
            device_id={"dom": lax.rem(dom + offsets[i], parts)}, device_id_type=MESH)

    def boundary_start(l):
        for i in (3, 0, 1, 2):
            copy = boundary(l, i)
            copy.start()
            started.append(copy)

    def step(l, s):
        for direction in range(2):
            ring_wait(l, direction, s)
        if s == 0:
            ring_start(l, 0, 2, left)
            ring_start(l, 1, 2, right)
        elif l + 1 < LAYERS:
            for direction in range(2):
                ring_start(l + 1, direction, s - 1, me)
        for direction in range(2):
            half = (direction if s != 1 else 1 - direction)
            hand_start(l, 2 * s + direction, piece(l, origin[direction][s], half))

    def block(l, j):
        x = jnp.concatenate([pools[l][codes[l, j, k]] for k in range(FAN)], axis=1)
        w = jnp.concatenate([wbufs[l][b, j] for b in range(SHARDS)], axis=0)
        summed = jnp.dot(x, w, preferred_element_type=jnp.float32)
        return jnp.maximum(summed + bias_v[j][l:l + 1], 0.0).astype(jnp.bfloat16)

    for copy in loads[:1 + BLK]:
        copy.wait()
    for s in range(2):
        for direction in range(2):
            ring_start(0, direction, s, me)
    hand_start(0, 6, wbufs[0].at[me])
    for i in (3, 0, 1, 2):
        stages[0][i] = first[sends[0, 0, i]]
    for copy in loads[1 + BLK:]:
        copy.wait()
    boundary_start(0)
    for l in range(1, LAYERS):
        hand_start(l, 6, wbufs[l].at[me])

    for l in range(LAYERS):
        for s in range(3):
            step(l, s)
        hand_wait(l)
        for i in range(NEIGH):
            boundary(l, i).wait_recv()
        if l + 1 < LAYERS:
            for i in (3, 0, 1, 2):
                stages[l + 1][i] = block(l, sends[l + 1, 0, i])
            boundary_start(l + 1)

            @pl.loop(0, BLK)
            def _(j):
                pools[l + 1][j] = block(l, j)
        else:
            def store(j):
                columns = pl.ds(pl.multiple_of(j * TILE, TILE), TILE)
                return pltpu.make_async_copy(final.at[j], out.at[:, columns], out_sem.at[j])

            @pl.loop(0, BLK)
            def _(j):
                final[j] = block(l, j)

                @pl.when(j > 0)
                def _():
                    store(j - 1).start()

            store(BLK - 1).start()
            for j in range(BLK):
                store(j).wait()
    for copy in started:
        copy.wait_send()


def body(activations, tile_weights, biases, source_codes, send_list):
    rows = activations.shape[0]
    parts = lax.axis_size("dom")
    part_rows = FAN * TILE // SHARDS
    anywhere = pl.BlockSpec(memory_space=pl.ANY)
    scalars = pl.BlockSpec(memory_space=pltpu.SMEM)
    dma = pltpu.SemaphoreType.DMA
    return pl.pallas_call(
        lambda *refs: kernel(parts, rows, *refs),
        out_shape=jax.ShapeDtypeStruct(activations.shape, jnp.bfloat16),
        in_specs=[anywhere, anywhere, anywhere, scalars, scalars],
        out_specs=anywhere,
        scratch_shapes=(
            [pltpu.VMEM((SHARDS, BLK, part_rows, TILE), jnp.bfloat16)] * LAYERS
            + [pltpu.VMEM((BLK + NEIGH, rows, TILE), jnp.bfloat16)] * LAYERS
            + [pltpu.VMEM((NEIGH, rows, TILE), jnp.bfloat16)] * LAYERS
            + [
                pltpu.VMEM((BLK, rows, TILE), jnp.bfloat16),
                pltpu.VMEM((BLK, rows, TILE), jnp.bfloat16),
                pltpu.VMEM((BLK, LAYERS, TILE), jnp.float32),
                dma((LAYERS, 2, 3)), dma((LAYERS, 2, 3)),
                dma((LAYERS, 7)), dma((LAYERS, 7)),
                dma((LAYERS, NEIGH)), dma((LAYERS, NEIGH)),
                dma((3 * BLK + LAYERS,)), dma((BLK,)),
            ]
        ),
        compiler_params=pltpu.CompilerParams(collective_id=0, has_side_effects=True),
        name="layers",
    )(activations, tile_weights, biases, source_codes, send_list)


def solution(mesh):
    in_specs = (
        P("batch", "dom"),
        P(None, "dom", "batch", None),
        P(None, "dom"),
        P(None, "dom", None),
        P(None, "dom", None),
    )
    out_specs = P("batch", "dom")
    return jax.shard_map(body, mesh=mesh, in_specs=in_specs, out_specs=out_specs, check_vma=False)
```

```python
import jax
import jax.numpy as jnp
from jax import lax
from jax.experimental import pallas as pl
from jax.experimental.pallas import tpu as pltpu
from jax.sharding import PartitionSpec as P

MESH = pl.DeviceIdType.MESH
LAYERS, BLK, FAN, TILE, NEIGH = 4, 16, 4, 128, 4
CHIPS, CORES = 4, 2
SHARDS = CHIPS * CORES
HALF = BLK // 2
GROUP = 4


def kernel(parts, rows, act, weights, biases, codes, sends, out, *scratch):
    wbufs, pools, stages = scratch[0:4], scratch[4:8], scratch[8:12]
    first, bias_v = scratch[12:14]
    xs_send, xs_recv, pt_send, pt_recv, bd_send, bd_recv, ld_sem = scratch[14:]

    dom = lax.axis_index("dom")
    me = lax.axis_index("batch")
    chip, core = me // CORES, me % CORES
    right = lax.rem(chip + 1, CHIPS) * CORES + core
    left = lax.rem(chip + CHIPS - 1, CHIPS) * CORES + core
    far = lax.rem(chip + 2, CHIPS) * CORES + core
    partner = chip * CORES + 1 - core
    offsets = (1, 2, parts - 1, parts // 2)

    loads = []

    def load(source, target):
        copy = pltpu.make_async_copy(source, target, ld_sem.at[len(loads)])
        copy.start()
        loads.append(copy)

    load(weights.at[0], wbufs[0].at[me])
    for j in range(BLK):
        load(act.at[:, pl.ds(j * TILE, TILE)], first.at[j])
    for l in range(1, LAYERS):
        load(weights.at[l], wbufs[l].at[me])
    for j in range(BLK):
        load(biases.at[:, pl.ds(j * TILE, TILE)], bias_v.at[j])
    for j in range(BLK):
        load(act.at[:, pl.ds(j * TILE, TILE)], pools[0].at[j])

    barrier = pltpu.get_barrier_semaphore()
    for peer in (left, right, partner):
        pl.semaphore_signal(barrier, inc=1, device_id={"batch": peer}, device_id_type=MESH)
    for offset in offsets:
        sender = lax.rem(dom + parts - offset, parts)
        pl.semaphore_signal(barrier, inc=1, device_id={"dom": sender}, device_id_type=MESH)
    pl.semaphore_wait(barrier, 7)

    started = []

    def piece(l, b, h):
        return wbufs[l].at[b, pl.ds(h * HALF, HALF)]

    def ring(l, direction, slot, b):
        half = (direction if slot != 1 else 1 - direction)
        ref = piece(l, b, half)
        return pltpu.make_async_remote_copy(
            src_ref=ref, dst_ref=ref,
            send_sem=xs_send.at[l, direction, slot], recv_sem=xs_recv.at[l, direction, slot],
            device_id={"batch": right if direction == 0 else left}, device_id_type=MESH)

    def ring_start(l, direction, slot, b):
        copy = ring(l, direction, slot, b)
        copy.start()
        started.append(copy)

    origin = ((left, left, far), (right, right, far))

    def ring_wait(l, direction, slot):
        ring(l, direction, slot, origin[direction][slot]).wait_recv()

    def hand(l, slot, ref):
        return pltpu.make_async_remote_copy(
            src_ref=ref, dst_ref=ref, send_sem=pt_send.at[l, slot], recv_sem=pt_recv.at[l, slot],
            device_id={"batch": partner}, device_id_type=MESH)

    def hand_start(l, slot, ref):
        copy = hand(l, slot, ref)
        copy.start()
        started.append(copy)

    def hand_wait(l):
        for slot in range(6):
            direction, s = slot % 2, slot // 2
            half = (direction if s != 1 else 1 - direction)
            b = origin[direction][s] + 1 - 2 * core
            hand(l, slot, piece(l, b, half)).wait_recv()
        hand(l, 6, wbufs[l].at[partner]).wait_recv()

    def boundary(l, i):
        return pltpu.make_async_remote_copy(
            src_ref=stages[l].at[i], dst_ref=pools[l].at[BLK + i],
            send_sem=bd_send.at[l, i], recv_sem=bd_recv.at[l, i],
            device_id={"dom": lax.rem(dom + offsets[i], parts)}, device_id_type=MESH)

    def boundary_start(l):
        for i in (3, 0, 1, 2):
            copy = boundary(l, i)
            copy.start()
            started.append(copy)

    def step(l, s):
        for direction in range(2):
            ring_wait(l, direction, s)
        if s == 0:
            ring_start(l, 0, 2, left)
            ring_start(l, 1, 2, right)
        elif l + 1 < LAYERS:
            for direction in range(2):
                ring_start(l + 1, direction, s - 1, me)
        for direction in range(2):
            half = (direction if s != 1 else 1 - direction)
            hand_start(l, 2 * s + direction, piece(l, origin[direction][s], half))

    def block(l, j):
        x = jnp.concatenate([pools[l][codes[l, k, j]] for k in range(FAN)], axis=1)
        w = jnp.concatenate([wbufs[l][b, j] for b in range(SHARDS)], axis=0)
        summed = jnp.dot(x, w, preferred_element_type=jnp.float32)
        return jnp.maximum(summed + bias_v[j][l:l + 1], 0.0).astype(jnp.bfloat16)

    for copy in loads[:1 + BLK]:
        copy.wait()
    for s in range(2):
        for direction in range(2):
            ring_start(0, direction, s, me)
    hand_start(0, 6, wbufs[0].at[me])
    for i in (3, 0, 1, 2):
        stages[0][i] = first[sends[0, 0, i]]
    for copy in loads[1 + BLK:]:
        copy.wait()
    boundary_start(0)
    for l in range(1, LAYERS):
        hand_start(l, 6, wbufs[l].at[me])

    for l in range(LAYERS):
        for s in range(3):
            step(l, s)
        hand_wait(l)
        for i in range(NEIGH):
            boundary(l, i).wait_recv()
        if l + 1 < LAYERS:
            early = [block(l, sends[l + 1, 0, i]) for i in range(NEIGH)]
            for i in range(NEIGH):
                stages[l + 1][i] = early[i]
            boundary_start(l + 1)

            @pl.loop(0, BLK // GROUP)
            def _(g):
                js = [g * GROUP + u for u in range(GROUP)]
                values = [block(l, j) for j in js]
                for j, value in zip(js, values):
                    pools[l + 1][j] = value
        else:
            @pl.loop(0, BLK // GROUP)
            def _(g):
                js = [g * GROUP + u for u in range(GROUP)]
                values = [block(l, j) for j in js]
                for j, value in zip(js, values):
                    out[j] = value

    for copy in started:
        copy.wait_send()


def spread(blocks, out, sem):
    copies = [
        pltpu.make_async_copy(blocks.at[j], out.at[:, pl.ds(j * TILE, TILE)], sem.at[j])
        for j in range(BLK)
    ]
    for copy in copies:
        copy.start()
    for copy in copies:
        copy.wait()


def body(activations, tile_weights, biases, source_codes, send_list):
    rows = activations.shape[0]
    parts = lax.axis_size("dom")
    part_rows = FAN * TILE // SHARDS
    anywhere = pl.BlockSpec(memory_space=pl.ANY)
    scalars = pl.BlockSpec(memory_space=pltpu.SMEM)
    dma = pltpu.SemaphoreType.DMA
    blocks = pl.pallas_call(
        lambda *refs: kernel(parts, rows, *refs),
        out_shape=pltpu.VMEM((BLK, rows, TILE), jnp.bfloat16),
        in_specs=[anywhere, anywhere, anywhere, scalars, scalars],
        out_specs=pl.BlockSpec(memory_space=pltpu.VMEM),
        scratch_shapes=(
            [pltpu.VMEM((SHARDS, BLK, part_rows, TILE), jnp.bfloat16)] * LAYERS
            + [pltpu.VMEM((BLK + NEIGH, rows, TILE), jnp.bfloat16)] * LAYERS
            + [pltpu.VMEM((NEIGH, rows, TILE), jnp.bfloat16)] * LAYERS
            + [
                pltpu.VMEM((BLK, rows, TILE), jnp.bfloat16),
                pltpu.VMEM((BLK, LAYERS, TILE), jnp.float32),
                dma((LAYERS, 2, 3)), dma((LAYERS, 2, 3)),
                dma((LAYERS, 7)), dma((LAYERS, 7)),
                dma((LAYERS, NEIGH)), dma((LAYERS, NEIGH)),
                dma((3 * BLK + LAYERS,)),
            ]
        ),
        compiler_params=pltpu.CompilerParams(collective_id=0, has_side_effects=True),
        name="layers",
    )(activations, tile_weights, biases, jnp.transpose(source_codes, (0, 2, 1)), send_list)
    return pl.pallas_call(
        spread,
        out_shape=jax.ShapeDtypeStruct(activations.shape, jnp.bfloat16),
        in_specs=[pl.BlockSpec(memory_space=pltpu.VMEM)],
        out_specs=anywhere,
        scratch_shapes=[dma((BLK,))],
        compiler_params=pltpu.CompilerParams(vmem_limit_bytes=4 << 20),
        name="spread",
    )(blocks)


def solution(mesh):
    in_specs = (
        P("batch", "dom"),
        P(None, "dom", "batch", None),
        P(None, "dom"),
        P(None, "dom", None),
        P(None, "dom", None),
    )
    out_specs = P("batch", "dom")
    return jax.shard_map(body, mesh=mesh, in_specs=in_specs, out_specs=out_specs, check_vma=False)
```

```python
import jax
import jax.numpy as jnp
from jax import lax
from jax.experimental import pallas as pl
from jax.experimental.pallas import tpu as pltpu
from jax.sharding import PartitionSpec as P

MESH = pl.DeviceIdType.MESH
LAYERS, BLK, FAN, TILE, NEIGH = 4, 16, 4, 128, 4
CHIPS, CORES = 4, 2
SHARDS = CHIPS * CORES
HALF = BLK // 2
GROUP = 4


def kernel(parts, rows, act, weights, biases, codes, sends, out, *scratch):
    wbufs, pools, stages = scratch[0:4], scratch[4:8], scratch[8:12]
    first, bias_v = scratch[12:14]
    xs_send, xs_recv, pt_send, pt_recv, bd_send, bd_recv, ld_sem, near, go = scratch[14:]

    dom = lax.axis_index("dom")
    me = lax.axis_index("batch")
    chip, core = me // CORES, me % CORES
    right = lax.rem(chip + 1, CHIPS) * CORES + core
    left = lax.rem(chip + CHIPS - 1, CHIPS) * CORES + core
    far = lax.rem(chip + 2, CHIPS) * CORES + core
    partner = chip * CORES + 1 - core
    offsets = (1, 2, parts - 1, parts // 2)

    barrier = pltpu.get_barrier_semaphore()

    def tell(semaphore, **peer):
        pl.semaphore_signal(semaphore, inc=1, device_id=peer, device_id_type=MESH)

    @pl.when(core == 0)
    def _():
        for peer in (left, right):
            tell(barrier, batch=peer)

    @pl.when(core == 1)
    def _():
        tell(barrier, batch=partner)

    loads = []

    def load(source, target):
        copy = pltpu.make_async_copy(source, target, ld_sem.at[len(loads)])
        copy.start()
        loads.append(copy)

    load(weights.at[0], wbufs[0].at[me])
    for j in range(BLK):
        load(act.at[:, pl.ds(j * TILE, TILE)], first.at[j])
    def piece(l, b, h):
        return wbufs[l].at[b, pl.ds(h * HALF, HALF)]

    def ring(l, direction, slot, b):
        half = (direction if slot != 1 else 1 - direction)
        ref = piece(l, b, half)
        return pltpu.make_async_remote_copy(
            src_ref=ref, dst_ref=ref,
            send_sem=xs_send.at[l, direction, slot], recv_sem=xs_recv.at[l, direction, slot],
            device_id={"batch": right if direction == 0 else left}, device_id_type=MESH)

    def ring_start(l, direction, slot, b):
        ring(l, direction, slot, b).start()

    origin = ((left, left, far), (right, right, far))

    def ring_wait(l, direction, slot):
        ring(l, direction, slot, origin[direction][slot]).wait_recv()

    def hand(l, slot, ref):
        return pltpu.make_async_remote_copy(
            src_ref=ref, dst_ref=ref, send_sem=pt_send.at[l, slot], recv_sem=pt_recv.at[l, slot],
            device_id={"batch": partner}, device_id_type=MESH)

    def hand_start(l, slot, ref):
        hand(l, slot, ref).start()

    def hand_wait(l):
        for slot in range(6):
            direction, s = slot % 2, slot // 2
            half = (direction if s != 1 else 1 - direction)
            b = origin[direction][s] + 1 - 2 * core
            hand(l, slot, piece(l, b, half)).wait_recv()
        hand(l, 6, wbufs[l].at[partner]).wait_recv()

    def boundary(l, i):
        return pltpu.make_async_remote_copy(
            src_ref=stages[l].at[i], dst_ref=pools[l].at[BLK + i],
            send_sem=bd_send.at[l, i], recv_sem=bd_recv.at[l, i],
            device_id={"dom": lax.rem(dom + offsets[i], parts)}, device_id_type=MESH)

    def boundary_start(l):
        for i in (3, 0, 1, 2):
            boundary(l, i).start()

    def ring_own(l):
        for slot in range(2):
            for direction in range(2):
                ring_start(l, direction, slot, me)

    def step(l, s):
        for direction in range(2):
            ring_wait(l, direction, s)
        if s == 0:
            ring_start(l, 0, 2, left)
            ring_start(l, 1, 2, right)
            if l + 1 < LAYERS:
                ring_own(l + 1)
        for direction in range(2):
            half = (direction if s != 1 else 1 - direction)
            hand_start(l, 2 * s + direction, piece(l, origin[direction][s], half))

    def block(l, j):
        x = jnp.concatenate([pools[l][codes[l, k, j]] for k in range(FAN)], axis=1)
        w = jnp.concatenate([wbufs[l][b, j] for b in range(SHARDS)], axis=0)
        summed = jnp.dot(x, w, preferred_element_type=jnp.float32)
        return jnp.maximum(summed + bias_v[j][l:l + 1], 0.0).astype(jnp.bfloat16)

    loads[0].wait()

    @pl.when(core == 0)
    def _():
        pl.semaphore_wait(barrier, 3)
        for peer in (left, right):
            tell(near, batch=peer)
        ring_own(0)
        hand_start(0, 6, wbufs[0].at[me])
        pl.semaphore_wait(near, 2)
        tell(go, batch=partner)

    @pl.when(core == 1)
    def _():
        pl.semaphore_wait(go, 1)
        for offset in offsets:
            tell(barrier, dom=lax.rem(dom + parts - offset, parts))
        ring_own(0)
        hand_start(0, 6, wbufs[0].at[me])

    for copy in loads[1:]:
        copy.wait()
    done = len(loads)
    for l in range(1, LAYERS):
        load(weights.at[l], wbufs[l].at[me])
    for j in range(BLK):
        load(biases.at[:, pl.ds(j * TILE, TILE)], bias_v.at[j])
    for j in range(BLK):
        load(act.at[:, pl.ds(j * TILE, TILE)], pools[0].at[j])
    for i in (3, 0, 1, 2):
        stages[0][i] = first[sends[0, 0, i]]
    for copy in loads[done:]:
        copy.wait()
    for l in range(1, LAYERS):
        hand_start(l, 6, wbufs[l].at[me])

    soon = dom < parts // 4
    step(0, 0)

    @pl.when(core == 1)
    def _():
        pl.semaphore_wait(barrier, NEIGH)
        tell(go, batch=partner)

    @pl.when(core == 0)
    def _():
        pl.semaphore_wait(go, 1)

    boundary_start(0)

    for l in range(LAYERS):
        if l > 0:
            @pl.when(jnp.logical_not(soon))
            def _():
                step(l, 0)
        step(l, 1)
        step(l, 2)
        if l + 1 < LAYERS:
            @pl.when(soon)
            def _():
                step(l + 1, 0)
        hand_wait(l)
        for i in range(NEIGH):
            boundary(l, i).wait_recv()
        if l + 1 < LAYERS:
            early = [block(l, sends[l + 1, 0, i]) for i in range(NEIGH)]
            for i in range(NEIGH):
                stages[l + 1][i] = early[i]
            boundary_start(l + 1)

            @pl.loop(0, BLK // GROUP)
            def _(g):
                js = [g * GROUP + u for u in range(GROUP)]
                values = [block(l, j) for j in js]
                for j, value in zip(js, values):
                    pools[l + 1][j] = value
        else:
            @pl.loop(0, BLK // GROUP)
            def _(g):
                js = [g * GROUP + u for u in range(GROUP)]
                values = [block(l, j) for j in js]
                for j, value in zip(js, values):
                    out[j] = value

    for l in range(LAYERS):
        for direction in range(2):
            for slot in range(3):
                b = me if slot < 2 else (left, right)[direction]
                ring(l, direction, slot, b).wait_send()
        for slot in range(6):
            direction, s = slot % 2, slot // 2
            half = (direction if s != 1 else 1 - direction)
            hand(l, slot, piece(l, origin[direction][s], half)).wait_send()
        hand(l, 6, wbufs[l].at[me]).wait_send()
        for i in range(NEIGH):
            boundary(l, i).wait_send()


def spread(blocks, out, sem):
    copies = [
        pltpu.make_async_copy(blocks.at[j], out.at[:, pl.ds(j * TILE, TILE)], sem.at[j])
        for j in range(BLK)
    ]
    for copy in copies:
        copy.start()
    for copy in copies:
        copy.wait()


def body(activations, tile_weights, biases, source_codes, send_list):
    rows = activations.shape[0]
    parts = lax.axis_size("dom")
    part_rows = FAN * TILE // SHARDS
    anywhere = pl.BlockSpec(memory_space=pl.ANY)
    scalars = pl.BlockSpec(memory_space=pltpu.SMEM)
    dma = pltpu.SemaphoreType.DMA
    blocks = pl.pallas_call(
        lambda *refs: kernel(parts, rows, *refs),
        out_shape=pltpu.VMEM((BLK, rows, TILE), jnp.bfloat16),
        in_specs=[anywhere, anywhere, anywhere, scalars, scalars],
        out_specs=pl.BlockSpec(memory_space=pltpu.VMEM),
        scratch_shapes=(
            [pltpu.VMEM((SHARDS, BLK, part_rows, TILE), jnp.bfloat16)] * LAYERS
            + [pltpu.VMEM((BLK + NEIGH, rows, TILE), jnp.bfloat16)] * LAYERS
            + [pltpu.VMEM((NEIGH, rows, TILE), jnp.bfloat16)] * LAYERS
            + [
                pltpu.VMEM((BLK, rows, TILE), jnp.bfloat16),
                pltpu.VMEM((BLK, LAYERS, TILE), jnp.float32),
                dma((LAYERS, 2, 3)), dma((LAYERS, 2, 3)),
                dma((LAYERS, 7)), dma((LAYERS, 7)),
                dma((LAYERS, NEIGH)), dma((LAYERS, NEIGH)),
                dma((3 * BLK + LAYERS,)),
                pltpu.SemaphoreType.REGULAR, pltpu.SemaphoreType.REGULAR,
            ]
        ),
        compiler_params=pltpu.CompilerParams(collective_id=0, has_side_effects=True),
        name="layers",
    )(activations, tile_weights, biases, jnp.transpose(source_codes, (0, 2, 1)), send_list)
    return pl.pallas_call(
        spread,
        out_shape=jax.ShapeDtypeStruct(activations.shape, jnp.bfloat16),
        in_specs=[pl.BlockSpec(memory_space=pltpu.VMEM)],
        out_specs=anywhere,
        scratch_shapes=[dma((BLK,))],
        compiler_params=pltpu.CompilerParams(vmem_limit_bytes=4 << 20),
        name="spread",
    )(blocks)


def solution(mesh):
    in_specs = (
        P("batch", "dom"),
        P(None, "dom", "batch", None),
        P(None, "dom"),
        P(None, "dom", None),
        P(None, "dom", None),
    )
    out_specs = P("batch", "dom")
    return jax.shard_map(body, mesh=mesh, in_specs=in_specs, out_specs=out_specs, check_vma=False)
```

```python
import jax
import jax.numpy as jnp
from jax import lax
from jax.experimental import pallas as pl
from jax.experimental.pallas import tpu as pltpu
from jax.sharding import PartitionSpec as P

MESH = pl.DeviceIdType.MESH
LAYERS, BLK, FAN, TILE, NEIGH = 4, 16, 4, 128, 4
CHIPS, CORES = 4, 2
SHARDS = CHIPS * CORES
HALF = BLK // 2
GROUP = 4
LAST_GROUP = 8


def kernel(parts, rows, act, weights, biases, codes, sends, out, *scratch):
    wbufs, stages = scratch[0:4], scratch[4:8]
    pools = [scratch[8:9], scratch[9:10], scratch[10:11], scratch[11:13]]
    first, bias_v = scratch[13:15]
    xs_send, xs_recv, pt_send, pt_recv, bd_send, bd_recv, ld_sem, near, go = scratch[15:]

    dom = lax.axis_index("dom")
    me = lax.axis_index("batch")
    chip, core = me // CORES, me % CORES
    right = lax.rem(chip + 1, CHIPS) * CORES + core
    left = lax.rem(chip + CHIPS - 1, CHIPS) * CORES + core
    far = lax.rem(chip + 2, CHIPS) * CORES + core
    partner = chip * CORES + 1 - core
    offsets = (1, 2, parts - 1, parts // 2)

    barrier = pltpu.get_barrier_semaphore()

    def tell(semaphore, **peer):
        pl.semaphore_signal(semaphore, inc=1, device_id=peer, device_id_type=MESH)

    @pl.when(core == 0)
    def _():
        for peer in (left, right):
            tell(barrier, batch=peer)

    @pl.when(core == 1)
    def _():
        tell(barrier, batch=partner)

    loads = []

    def load(source, target):
        copy = pltpu.make_async_copy(source, target, ld_sem.at[len(loads)])
        copy.start()
        loads.append(copy)

    load(weights.at[0], wbufs[0].at[me])
    for j in range(BLK):
        load(act.at[:, pl.ds(j * TILE, TILE)], first.at[j])
    def piece(l, b, h):
        return wbufs[l].at[b, pl.ds(h * HALF, HALF)]

    def ring(l, direction, slot, b):
        half = (direction if slot != 1 else 1 - direction)
        ref = piece(l, b, half)
        return pltpu.make_async_remote_copy(
            src_ref=ref, dst_ref=ref,
            send_sem=xs_send.at[l, direction, slot], recv_sem=xs_recv.at[l, direction, slot],
            device_id={"batch": right if direction == 0 else left}, device_id_type=MESH)

    def ring_start(l, direction, slot, b):
        ring(l, direction, slot, b).start()

    origin = ((left, left, far), (right, right, far))

    def ring_wait(l, direction, slot):
        ring(l, direction, slot, origin[direction][slot]).wait_recv()

    def hand(l, slot, ref):
        return pltpu.make_async_remote_copy(
            src_ref=ref, dst_ref=ref, send_sem=pt_send.at[l, slot], recv_sem=pt_recv.at[l, slot],
            device_id={"batch": partner}, device_id_type=MESH)

    def hand_start(l, slot, ref):
        hand(l, slot, ref).start()

    def hand_wait(l):
        for slot in range(6):
            direction, s = slot % 2, slot // 2
            half = (direction if s != 1 else 1 - direction)
            b = origin[direction][s] + 1 - 2 * core
            hand(l, slot, piece(l, b, half)).wait_recv()
        hand(l, 6, wbufs[l].at[partner]).wait_recv()

    def boundary(l, i, part):
        count = rows // len(pools[l])
        return pltpu.make_async_remote_copy(
            src_ref=stages[l].at[i, pl.ds(part * count, count)], dst_ref=pools[l][part].at[BLK + i],
            send_sem=bd_send.at[l, i, part], recv_sem=bd_recv.at[l, i, part],
            device_id={"dom": lax.rem(dom + offsets[i], parts)}, device_id_type=MESH)

    def boundary_start(l, part):
        @pl.when(last)
        def _():
            for i in (0, 1, 3, 2):
                boundary(l, i, part).start()

        @pl.when(jnp.logical_not(last))
        def _():
            for i in (3, 0, 1, 2):
                boundary(l, i, part).start()

    def boundary_wait(l, part):
        for i in range(NEIGH):
            boundary(l, i, part).wait_recv()

    def ring_own(l):
        for slot in range(2):
            for direction in range(2):
                ring_start(l, direction, slot, me)

    def step(l, s):
        for direction in range(2):
            ring_wait(l, direction, s)
        if s == 0:
            ring_start(l, 0, 2, left)
            ring_start(l, 1, 2, right)
            if l + 1 < LAYERS:
                ring_own(l + 1)
        for direction in range(2):
            half = (direction if s != 1 else 1 - direction)
            hand_start(l, 2 * s + direction, piece(l, origin[direction][s], half))

    def block(l, j, part, start, count):
        pool = pools[l][part]
        x = jnp.concatenate([pool[codes[l, k, j], pl.ds(start, count)] for k in range(FAN)], axis=1)
        w = jnp.concatenate([wbufs[l][b, j] for b in range(SHARDS)], axis=0)
        summed = jnp.dot(x, w, preferred_element_type=jnp.float32)
        return jnp.maximum(summed + bias_v[j][l:l + 1], 0.0).astype(jnp.bfloat16)

    loads[0].wait()

    @pl.when(core == 0)
    def _():
        pl.semaphore_wait(barrier, 3)
        for peer in (left, right):
            tell(near, batch=peer)
        ring_own(0)
        hand_start(0, 6, wbufs[0].at[me])
        pl.semaphore_wait(near, 2)
        tell(go, batch=partner)

    @pl.when(core == 1)
    def _():
        pl.semaphore_wait(go, 1)
        for offset in offsets:
            tell(barrier, dom=lax.rem(dom + parts - offset, parts))
        ring_own(0)
        hand_start(0, 6, wbufs[0].at[me])

    for copy in loads[1:]:
        copy.wait()
    done = len(loads)
    for l in range(1, LAYERS):
        load(weights.at[l], wbufs[l].at[me])
    for j in range(BLK):
        load(biases.at[:, pl.ds(j * TILE, TILE)], bias_v.at[j])
    for j in range(BLK):
        load(act.at[:, pl.ds(j * TILE, TILE)], pools[0][0].at[j])
    for i in (3, 0, 1, 2):
        stages[0][i] = first[sends[0, 0, i]]
    for copy in loads[done:]:
        copy.wait()
    for l in range(1, LAYERS):
        hand_start(l, 6, wbufs[l].at[me])

    soon = dom < parts // 4
    last = dom >= parts - 4
    step(0, 0)

    @pl.when(core == 1)
    def _():
        pl.semaphore_wait(barrier, NEIGH)
        tell(go, batch=partner)

    @pl.when(core == 0)
    def _():
        pl.semaphore_wait(go, 1)

    boundary_start(0, 0)

    for l in range(LAYERS):
        step(l, 1)
        step(l, 2)
        if l + 1 < LAYERS:
            @pl.when(soon)
            def _():
                step(l + 1, 0)
        hand_wait(l)
        if l + 1 < LAYERS:
            boundary_wait(l, 0)
            count = rows // len(pools[l + 1])
            for part in range(len(pools[l + 1])):
                early = [block(l, sends[l + 1, 0, i], 0, part * count, count) for i in range(NEIGH)]
                for i in range(NEIGH):
                    stages[l + 1][i, pl.ds(part * count, count)] = early[i]
                boundary_start(l + 1, part)

            @pl.when(jnp.logical_not(soon))
            def _():
                step(l + 1, 0)

            @pl.loop(0, BLK // GROUP)
            def _(g):
                js = [g * GROUP + u for u in range(GROUP)]
                values = [block(l, j, 0, 0, rows) for j in js]
                for j, value in zip(js, values):
                    for part in range(len(pools[l + 1])):
                        pools[l + 1][part][j] = value[part * count:(part + 1) * count]
        else:
            count = rows // len(pools[l])
            for part in range(len(pools[l])):
                boundary_wait(l, part)

                @pl.loop(0, BLK // LAST_GROUP)
                def _(g):
                    js = [g * LAST_GROUP + u for u in range(LAST_GROUP)]
                    values = [block(l, j, part, 0, count) for j in js]
                    for j, value in zip(js, values):
                        columns = pl.ds(pl.multiple_of(j * TILE, TILE), TILE)
                        out[pl.ds(part * count, count), columns] = value

    for l in range(LAYERS):
        for direction in range(2):
            for slot in range(3):
                b = me if slot < 2 else (left, right)[direction]
                ring(l, direction, slot, b).wait_send()
        for slot in range(6):
            direction, s = slot % 2, slot // 2
            half = (direction if s != 1 else 1 - direction)
            hand(l, slot, piece(l, origin[direction][s], half)).wait_send()
        hand(l, 6, wbufs[l].at[me]).wait_send()
        for part in range(len(pools[l])):
            for i in range(NEIGH):
                boundary(l, i, part).wait_send()


def body(activations, tile_weights, biases, source_codes, send_list):
    rows = activations.shape[0]
    parts = lax.axis_size("dom")
    part_rows = FAN * TILE // SHARDS
    anywhere = pl.BlockSpec(memory_space=pl.ANY)
    scalars = pl.BlockSpec(memory_space=pltpu.SMEM)
    dma = pltpu.SemaphoreType.DMA
    return pl.pallas_call(
        lambda *refs: kernel(parts, rows, *refs),
        out_shape=pltpu.VMEM((rows, BLK * TILE), jnp.bfloat16),
        in_specs=[anywhere, anywhere, anywhere, scalars, scalars],
        out_specs=pl.BlockSpec(memory_space=pltpu.VMEM),
        scratch_shapes=(
            [pltpu.VMEM((SHARDS, BLK, part_rows, TILE), jnp.bfloat16)] * LAYERS
            + [pltpu.VMEM((NEIGH, rows, TILE), jnp.bfloat16)] * LAYERS
            + [pltpu.VMEM((BLK + NEIGH, rows, TILE), jnp.bfloat16)] * (LAYERS - 1)
            + [pltpu.VMEM((BLK + NEIGH, rows // 2, TILE), jnp.bfloat16)] * 2
            + [
                pltpu.VMEM((BLK, rows, TILE), jnp.bfloat16),
                pltpu.VMEM((BLK, LAYERS, TILE), jnp.float32),
                dma((LAYERS, 2, 3)), dma((LAYERS, 2, 3)),
                dma((LAYERS, 7)), dma((LAYERS, 7)),
                dma((LAYERS, NEIGH, 2)), dma((LAYERS, NEIGH, 2)),
                dma((3 * BLK + LAYERS,)),
                pltpu.SemaphoreType.REGULAR, pltpu.SemaphoreType.REGULAR,
            ]
        ),
        compiler_params=pltpu.CompilerParams(collective_id=0, has_side_effects=True),
        name="layers",
    )(activations, tile_weights, biases, jnp.transpose(source_codes, (0, 2, 1)), send_list)


def solution(mesh):
    in_specs = (
        P("batch", "dom"),
        P(None, "dom", "batch", None),
        P(None, "dom"),
        P(None, "dom", None),
        P(None, "dom", None),
    )
    out_specs = P("batch", "dom")
    return jax.shard_map(body, mesh=mesh, in_specs=in_specs, out_specs=out_specs, check_vma=False)
```

```python
import jax
import jax.numpy as jnp
from jax import lax
from jax.experimental import pallas as pl
from jax.experimental.pallas import tpu as pltpu
from jax.sharding import PartitionSpec as P

MESH = pl.DeviceIdType.MESH
LAYERS, BLK, FAN, TILE, NEIGH = 4, 16, 4, 128, 4
CHIPS, CORES = 4, 2
SHARDS = CHIPS * CORES
HALF = BLK // 2
GROUP = 4
LAST_GROUP = 8


def kernel(parts, rows, act, weights, biases, codes_in, sends_in, out, *scratch):
    wbufs, stages = scratch[0:4], scratch[4:8]
    pools = [scratch[8:9], scratch[9:10], scratch[10:11], scratch[11:13]]
    first, bias_v = scratch[13:15]
    xs_send, xs_recv, pt_send, pt_recv, bd_send, bd_recv, ld_sem, near, go, codes, sends = scratch[15:]

    dom = lax.axis_index("dom")
    me = lax.axis_index("batch")
    chip, core = me // CORES, me % CORES
    right = lax.rem(chip + 1, CHIPS) * CORES + core
    left = lax.rem(chip + CHIPS - 1, CHIPS) * CORES + core
    far = lax.rem(chip + 2, CHIPS) * CORES + core
    partner = chip * CORES + 1 - core
    offsets = (1, 2, parts - 1, parts // 2)

    barrier = pltpu.get_barrier_semaphore()

    def tell(semaphore, **peer):
        pl.semaphore_signal(semaphore, inc=1, device_id=peer, device_id_type=MESH)

    @pl.when(core == 0)
    def _():
        for peer in (left, right):
            tell(barrier, batch=peer)

    @pl.when(core == 1)
    def _():
        tell(barrier, batch=partner)

    loads = []

    def load(source, target):
        copy = pltpu.make_async_copy(source, target, ld_sem.at[len(loads)])
        copy.start()
        loads.append(copy)

    load(weights.at[0], wbufs[0].at[me])
    load(codes_in, codes)
    load(sends_in, sends)
    for j in range(BLK):
        load(act.at[:, pl.ds(j * TILE, TILE)], first.at[j])
    def piece(l, b, h):
        return wbufs[l].at[b, pl.ds(h * HALF, HALF)]

    def ring(l, direction, slot, b):
        half = (direction if slot != 1 else 1 - direction)
        ref = piece(l, b, half)
        return pltpu.make_async_remote_copy(
            src_ref=ref, dst_ref=ref,
            send_sem=xs_send.at[l, direction, slot], recv_sem=xs_recv.at[l, direction, slot],
            device_id={"batch": right if direction == 0 else left}, device_id_type=MESH)

    def ring_start(l, direction, slot, b):
        ring(l, direction, slot, b).start()

    origin = ((left, left, far), (right, right, far))

    def ring_wait(l, direction, slot):
        ring(l, direction, slot, origin[direction][slot]).wait_recv()

    def hand(l, slot, ref):
        return pltpu.make_async_remote_copy(
            src_ref=ref, dst_ref=ref, send_sem=pt_send.at[l, slot], recv_sem=pt_recv.at[l, slot],
            device_id={"batch": partner}, device_id_type=MESH)

    def hand_start(l, slot, ref):
        hand(l, slot, ref).start()

    def hand_wait(l):
        for slot in range(6):
            direction, s = slot % 2, slot // 2
            half = (direction if s != 1 else 1 - direction)
            b = origin[direction][s] + 1 - 2 * core
            hand(l, slot, piece(l, b, half)).wait_recv()
        hand(l, 6, wbufs[l].at[partner]).wait_recv()

    def boundary(l, i, part):
        count = rows // len(pools[l])
        return pltpu.make_async_remote_copy(
            src_ref=stages[l].at[i, pl.ds(part * count, count)], dst_ref=pools[l][part].at[BLK + i],
            send_sem=bd_send.at[l, i, part], recv_sem=bd_recv.at[l, i, part],
            device_id={"dom": lax.rem(dom + offsets[i], parts)}, device_id_type=MESH)

    def boundary_start(l, part):
        @pl.when(last)
        def _():
            for i in (0, 1, 3, 2):
                boundary(l, i, part).start()

        @pl.when(jnp.logical_not(last))
        def _():
            for i in (3, 0, 1, 2):
                boundary(l, i, part).start()

    def boundary_wait(l, part):
        for i in range(NEIGH):
            boundary(l, i, part).wait_recv()

    def ring_own(l):
        for slot in range(2):
            for direction in range(2):
                ring_start(l, direction, slot, me)

    def step(l, s):
        for direction in range(2):
            ring_wait(l, direction, s)
        if s == 0:
            ring_start(l, 0, 2, left)
            ring_start(l, 1, 2, right)
            if l + 1 < LAYERS:
                ring_own(l + 1)
        for direction in range(2):
            half = (direction if s != 1 else 1 - direction)
            hand_start(l, 2 * s + direction, piece(l, origin[direction][s], half))

    def block(l, j, part, start, count):
        pool = pools[l][part]
        x = jnp.concatenate([pool[codes[l, k, j], pl.ds(start, count)] for k in range(FAN)], axis=1)
        w = jnp.concatenate([wbufs[l][b, j] for b in range(SHARDS)], axis=0)
        summed = jnp.dot(x, w, preferred_element_type=jnp.float32)
        return jnp.maximum(summed + bias_v[j][l:l + 1], 0.0).astype(jnp.bfloat16)

    loads[0].wait()

    @pl.when(core == 0)
    def _():
        pl.semaphore_wait(barrier, 3)
        for peer in (left, right):
            tell(near, batch=peer)
        ring_own(0)
        hand_start(0, 6, wbufs[0].at[me])
        pl.semaphore_wait(near, 2)
        tell(go, batch=partner)

    @pl.when(core == 1)
    def _():
        pl.semaphore_wait(go, 1)
        for offset in offsets:
            tell(barrier, dom=lax.rem(dom + parts - offset, parts))
        ring_own(0)
        hand_start(0, 6, wbufs[0].at[me])

    for copy in loads[1:]:
        copy.wait()
    done = len(loads)
    for l in range(1, LAYERS):
        load(weights.at[l], wbufs[l].at[me])
    for j in range(BLK):
        load(biases.at[:, pl.ds(j * TILE, TILE)], bias_v.at[j])
    for j in range(BLK):
        load(act.at[:, pl.ds(j * TILE, TILE)], pools[0][0].at[j])
    for i in (3, 0, 1, 2):
        stages[0][i] = first[sends[0, 0, i]]
    for copy in loads[done:]:
        copy.wait()
    for l in range(1, LAYERS):
        hand_start(l, 6, wbufs[l].at[me])

    soon = dom < parts // 4
    last = dom >= parts - 4
    step(0, 0)

    @pl.when(core == 1)
    def _():
        pl.semaphore_wait(barrier, NEIGH)
        tell(go, batch=partner)

    @pl.when(core == 0)
    def _():
        pl.semaphore_wait(go, 1)

    boundary_start(0, 0)

    for l in range(LAYERS):
        step(l, 1)
        step(l, 2)
        if l + 1 < LAYERS:
            @pl.when(soon)
            def _():
                step(l + 1, 0)
        hand_wait(l)
        if l + 1 < LAYERS:
            boundary_wait(l, 0)
            count = rows // len(pools[l + 1])
            for part in range(len(pools[l + 1])):
                early = [block(l, sends[l + 1, 0, i], 0, part * count, count) for i in range(NEIGH)]
                for i in range(NEIGH):
                    stages[l + 1][i, pl.ds(part * count, count)] = early[i]
                boundary_start(l + 1, part)

            @pl.when(jnp.logical_not(soon))
            def _():
                step(l + 1, 0)

            @pl.loop(0, BLK // GROUP)
            def _(g):
                js = [g * GROUP + u for u in range(GROUP)]
                values = [block(l, j, 0, 0, rows) for j in js]
                for j, value in zip(js, values):
                    for part in range(len(pools[l + 1])):
                        pools[l + 1][part][j] = value[part * count:(part + 1) * count]
        else:
            count = rows // len(pools[l])
            for part in range(len(pools[l])):
                boundary_wait(l, part)

                @pl.loop(0, BLK // LAST_GROUP)
                def _(g):
                    js = [g * LAST_GROUP + u for u in range(LAST_GROUP)]
                    values = [block(l, j, part, 0, count) for j in js]
                    for j, value in zip(js, values):
                        columns = pl.ds(pl.multiple_of(j * TILE, TILE), TILE)
                        out[pl.ds(part * count, count), columns] = value

    for l in range(LAYERS):
        for direction in range(2):
            for slot in range(3):
                b = me if slot < 2 else (left, right)[direction]
                ring(l, direction, slot, b).wait_send()
        for slot in range(6):
            direction, s = slot % 2, slot // 2
            half = (direction if s != 1 else 1 - direction)
            hand(l, slot, piece(l, origin[direction][s], half)).wait_send()
        hand(l, 6, wbufs[l].at[me]).wait_send()
        for part in range(len(pools[l])):
            for i in range(NEIGH):
                boundary(l, i, part).wait_send()


def body(activations, tile_weights, biases, source_codes, send_list):
    rows = activations.shape[0]
    parts = lax.axis_size("dom")
    part_rows = FAN * TILE // SHARDS
    anywhere = pl.BlockSpec(memory_space=pl.ANY)
    dma = pltpu.SemaphoreType.DMA
    return pl.pallas_call(
        lambda *refs: kernel(parts, rows, *refs),
        out_shape=pltpu.VMEM((rows, BLK * TILE), jnp.bfloat16),
        in_specs=[anywhere] * 5,
        out_specs=pl.BlockSpec(memory_space=pltpu.VMEM),
        scratch_shapes=(
            [pltpu.VMEM((SHARDS, BLK, part_rows, TILE), jnp.bfloat16)] * LAYERS
            + [pltpu.VMEM((NEIGH, rows, TILE), jnp.bfloat16)] * LAYERS
            + [pltpu.VMEM((BLK + NEIGH, rows, TILE), jnp.bfloat16)] * (LAYERS - 1)
            + [pltpu.VMEM((BLK + NEIGH, rows // 2, TILE), jnp.bfloat16)] * 2
            + [
                pltpu.VMEM((BLK, rows, TILE), jnp.bfloat16),
                pltpu.VMEM((BLK, LAYERS, TILE), jnp.float32),
                dma((LAYERS, 2, 3)), dma((LAYERS, 2, 3)),
                dma((LAYERS, 7)), dma((LAYERS, 7)),
                dma((LAYERS, NEIGH, 2)), dma((LAYERS, NEIGH, 2)),
                dma((3 * BLK + LAYERS + 2,)),
                pltpu.SemaphoreType.REGULAR, pltpu.SemaphoreType.REGULAR,
                pltpu.SMEM(source_codes.shape[:1] + source_codes.shape[:0:-1], jnp.int32), pltpu.SMEM(send_list.shape, jnp.int32),
            ]
        ),
        compiler_params=pltpu.CompilerParams(collective_id=0, has_side_effects=True),
        name="layers",
    )(activations, tile_weights, biases, jnp.transpose(source_codes, (0, 2, 1)), send_list)


def solution(mesh):
    in_specs = (
        P("batch", "dom"),
        P(None, "dom", "batch", None),
        P(None, "dom"),
        P(None, "dom", None),
        P(None, "dom", None),
    )
    out_specs = P("batch", "dom")
    return jax.shard_map(body, mesh=mesh, in_specs=in_specs, out_specs=out_specs, check_vma=False)
```

```python
import jax
import jax.numpy as jnp
from jax import lax
from jax.experimental import pallas as pl
from jax.experimental.pallas import tpu as pltpu
from jax.sharding import PartitionSpec as P

MESH = pl.DeviceIdType.MESH
LAYERS, BLK, FAN, TILE, NEIGH = 4, 16, 4, 128, 4
CHIPS, CORES = 4, 2
SHARDS = CHIPS * CORES
HALF = BLK // 2
GROUP = 4
LAST_GROUP = 8


def kernel(parts, rows, act, weights, biases, codes_in, sends_in, out, *scratch):
    wbufs, stages = scratch[0:4], scratch[4:8]
    pools = [scratch[8:9], scratch[9:10], scratch[10:11], scratch[11:13]]
    first, bias_v = scratch[13:15]
    xs_send, xs_recv, pt_send, pt_recv, bd_send, bd_recv, ld_sem, near, go, codes, sends = scratch[15:]

    dom = lax.axis_index("dom")
    me = lax.axis_index("batch")
    chip, core = me // CORES, me % CORES
    right = lax.rem(chip + 1, CHIPS) * CORES + core
    left = lax.rem(chip + CHIPS - 1, CHIPS) * CORES + core
    far = lax.rem(chip + 2, CHIPS) * CORES + core
    partner = chip * CORES + 1 - core
    offsets = (1, 2, parts - 1, parts // 2)

    barrier = pltpu.get_barrier_semaphore()

    def tell(semaphore, **peer):
        pl.semaphore_signal(semaphore, inc=1, device_id=peer, device_id_type=MESH)

    @pl.when(core == 0)
    def _():
        for peer in (left, right):
            tell(barrier, batch=peer)

    @pl.when(core == 1)
    def _():
        tell(barrier, batch=partner)

    loads = []

    def load(source, target):
        copy = pltpu.make_async_copy(source, target, ld_sem.at[len(loads)])
        copy.start()
        loads.append(copy)

    load(weights.at[0], wbufs[0].at[me])
    load(codes_in, codes)
    load(sends_in, sends)
    for j in range(BLK):
        load(act.at[:, pl.ds(j * TILE, TILE)], first.at[j])
    def piece(l, b, h):
        return wbufs[l].at[b, pl.ds(h * HALF, HALF)]

    def ring(l, direction, slot, b):
        half = (direction if slot != 1 else 1 - direction)
        ref = piece(l, b, half)
        return pltpu.make_async_remote_copy(
            src_ref=ref, dst_ref=ref,
            send_sem=xs_send.at[l, direction, slot], recv_sem=xs_recv.at[l, direction, slot],
            device_id={"batch": right if direction == 0 else left}, device_id_type=MESH)

    def ring_start(l, direction, slot, b):
        ring(l, direction, slot, b).start()

    origin = ((left, left, far), (right, right, far))

    def ring_wait(l, direction, slot):
        ring(l, direction, slot, origin[direction][slot]).wait_recv()

    def hand(l, slot, ref):
        return pltpu.make_async_remote_copy(
            src_ref=ref, dst_ref=ref, send_sem=pt_send.at[l, slot], recv_sem=pt_recv.at[l, slot],
            device_id={"batch": partner}, device_id_type=MESH)

    def hand_start(l, slot, ref):
        hand(l, slot, ref).start()

    def hand_wait(l):
        for slot in range(6):
            direction, s = slot % 2, slot // 2
            half = (direction if s != 1 else 1 - direction)
            b = origin[direction][s] + 1 - 2 * core
            hand(l, slot, piece(l, b, half)).wait_recv()
        hand(l, 6, wbufs[l].at[partner]).wait_recv()

    def boundary(l, i, part):
        count = rows // len(pools[l])
        return pltpu.make_async_remote_copy(
            src_ref=stages[l].at[i, pl.ds(part * count, count)], dst_ref=pools[l][part].at[BLK + i],
            send_sem=bd_send.at[l, i, part], recv_sem=bd_recv.at[l, i, part],
            device_id={"dom": lax.rem(dom + offsets[i], parts)}, device_id_type=MESH)

    def boundary_start(l, part):
        @pl.when(last)
        def _():
            for i in (0, 1, 3, 2):
                boundary(l, i, part).start()

        @pl.when(jnp.logical_not(last))
        def _():
            for i in (3, 0, 1, 2):
                boundary(l, i, part).start()

    def boundary_wait(l, part):
        for i in range(NEIGH):
            boundary(l, i, part).wait_recv()

    def ring_own(l):
        for slot in range(2):
            for direction in range(2):
                ring_start(l, direction, slot, me)

    def step(l, s):
        for direction in range(2):
            ring_wait(l, direction, s)
        if s == 0:
            ring_start(l, 0, 2, left)
            ring_start(l, 1, 2, right)
            if l + 1 < LAYERS:
                ring_own(l + 1)
        for direction in range(2):
            half = (direction if s != 1 else 1 - direction)
            hand_start(l, 2 * s + direction, piece(l, origin[direction][s], half))

    def block(l, j, part, start, count):
        pool = pools[l][part]
        x = jnp.concatenate([pool[codes[l, k, j], pl.ds(start, count)] for k in range(FAN)], axis=1)
        w = jnp.concatenate([wbufs[l][b, j] for b in range(SHARDS)], axis=0)
        summed = jnp.dot(x, w, preferred_element_type=jnp.float32)
        return jnp.maximum(summed + bias_v[j][l:l + 1], 0.0).astype(jnp.bfloat16)

    def sent(l):
        for direction in range(2):
            for slot in range(3):
                b = me if slot < 2 else (left, right)[direction]
                ring(l, direction, slot, b).wait_send()
        for slot in range(6):
            direction, s = slot % 2, slot // 2
            half = (direction if s != 1 else 1 - direction)
            hand(l, slot, piece(l, origin[direction][s], half)).wait_send()
        hand(l, 6, wbufs[l].at[me]).wait_send()
        for part in range(len(pools[l])):
            for i in range(NEIGH):
                boundary(l, i, part).wait_send()

    loads[0].wait()

    @pl.when(core == 0)
    def _():
        pl.semaphore_wait(barrier, 3)
        for peer in (left, right):
            tell(near, batch=peer)
        ring_own(0)
        hand_start(0, 6, wbufs[0].at[me])
        pl.semaphore_wait(near, 2)
        tell(go, batch=partner)

    @pl.when(core == 1)
    def _():
        pl.semaphore_wait(go, 1)
        for offset in offsets:
            tell(barrier, dom=lax.rem(dom + parts - offset, parts))
        ring_own(0)
        hand_start(0, 6, wbufs[0].at[me])

    for copy in loads[1:]:
        copy.wait()
    done = len(loads)
    for l in range(1, LAYERS):
        load(weights.at[l], wbufs[l].at[me])
    for j in range(BLK):
        load(biases.at[:, pl.ds(j * TILE, TILE)], bias_v.at[j])
    for j in range(BLK):
        load(act.at[:, pl.ds(j * TILE, TILE)], pools[0][0].at[j])
    for i in (3, 0, 1, 2):
        stages[0][i] = first[sends[0, 0, i]]
    for copy in loads[done:]:
        copy.wait()
    for l in range(1, LAYERS):
        hand_start(l, 6, wbufs[l].at[me])

    soon = dom < parts // 4
    last = dom >= parts - 4
    step(0, 0)

    @pl.when(core == 1)
    def _():
        pl.semaphore_wait(barrier, NEIGH)
        tell(go, batch=partner)

    @pl.when(core == 0)
    def _():
        pl.semaphore_wait(go, 1)

    boundary_start(0, 0)

    for l in range(LAYERS):
        step(l, 1)
        step(l, 2)
        if l + 1 < LAYERS:
            @pl.when(soon)
            def _():
                step(l + 1, 0)
        hand_wait(l)
        if l + 1 < LAYERS:
            boundary_wait(l, 0)
            count = rows // len(pools[l + 1])
            for part in range(len(pools[l + 1])):
                early = [block(l, sends[l + 1, 0, i], 0, part * count, count) for i in range(NEIGH)]
                for i in range(NEIGH):
                    stages[l + 1][i, pl.ds(part * count, count)] = early[i]
                boundary_start(l + 1, part)

            @pl.when(jnp.logical_not(soon))
            def _():
                step(l + 1, 0)

            @pl.loop(0, BLK // GROUP)
            def _(g):
                js = [g * GROUP + u for u in range(GROUP)]
                values = [block(l, j, 0, 0, rows) for j in js]
                for j, value in zip(js, values):
                    for part in range(len(pools[l + 1])):
                        pools[l + 1][part][j] = value[part * count:(part + 1) * count]
        else:
            count = rows // len(pools[l])
            for layer in range(LAYERS - 1):
                sent(layer)
            for part in range(len(pools[l])):
                boundary_wait(l, part)

                @pl.loop(0, BLK // LAST_GROUP)
                def _(g):
                    js = [g * LAST_GROUP + u for u in range(LAST_GROUP)]
                    values = [block(l, j, part, 0, count) for j in js]
                    for j, value in zip(js, values):
                        columns = pl.ds(pl.multiple_of(j * TILE, TILE), TILE)
                        out[pl.ds(part * count, count), columns] = value
    sent(LAYERS - 1)


def body(activations, tile_weights, biases, source_codes, send_list):
    rows = activations.shape[0]
    parts = lax.axis_size("dom")
    part_rows = FAN * TILE // SHARDS
    anywhere = pl.BlockSpec(memory_space=pl.ANY)
    dma = pltpu.SemaphoreType.DMA
    return pl.pallas_call(
        lambda *refs: kernel(parts, rows, *refs),
        out_shape=pltpu.VMEM((rows, BLK * TILE), jnp.bfloat16),
        in_specs=[anywhere] * 5,
        out_specs=pl.BlockSpec(memory_space=pltpu.VMEM),
        scratch_shapes=(
            [pltpu.VMEM((SHARDS, BLK, part_rows, TILE), jnp.bfloat16)] * LAYERS
            + [pltpu.VMEM((NEIGH, rows, TILE), jnp.bfloat16)] * LAYERS
            + [pltpu.VMEM((BLK + NEIGH, rows, TILE), jnp.bfloat16)] * (LAYERS - 1)
            + [pltpu.VMEM((BLK + NEIGH, rows // 2, TILE), jnp.bfloat16)] * 2
            + [
                pltpu.VMEM((BLK, rows, TILE), jnp.bfloat16),
                pltpu.VMEM((BLK, LAYERS, TILE), jnp.float32),
                dma((LAYERS, 2, 3)), dma((LAYERS, 2, 3)),
                dma((LAYERS, 7)), dma((LAYERS, 7)),
                dma((LAYERS, NEIGH, 2)), dma((LAYERS, NEIGH, 2)),
                dma((3 * BLK + LAYERS + 2,)),
                pltpu.SemaphoreType.REGULAR, pltpu.SemaphoreType.REGULAR,
                pltpu.SMEM(source_codes.shape[:1] + source_codes.shape[:0:-1], jnp.int32), pltpu.SMEM(send_list.shape, jnp.int32),
            ]
        ),
        compiler_params=pltpu.CompilerParams(collective_id=0, has_side_effects=True),
        name="layers",
    )(activations, tile_weights, biases, jnp.transpose(source_codes, (0, 2, 1)), send_list)


def solution(mesh):
    in_specs = (
        P("batch", "dom"),
        P(None, "dom", "batch", None),
        P(None, "dom"),
        P(None, "dom", None),
        P(None, "dom", None),
    )
    out_specs = P("batch", "dom")
    return jax.shard_map(body, mesh=mesh, in_specs=in_specs, out_specs=out_specs, check_vma=False)
```

```python
import jax
import jax.numpy as jnp
from jax import lax
from jax.experimental import pallas as pl
from jax.experimental.pallas import tpu as pltpu
from jax.sharding import PartitionSpec as P

MESH = pl.DeviceIdType.MESH
LAYERS, BLK, FAN, TILE, NEIGH = 4, 16, 4, 128, 4
CHIPS, CORES = 4, 2
SHARDS = CHIPS * CORES
HALF = BLK // 2
SUBS = 2
SLOTS = 2 + SUBS
GROUP = 4
LAST_GROUP = 16


def kernel(parts, rows, act, weights, biases, codes_in, sends_in, out, *scratch):
    wbufs, stages = scratch[0:4], scratch[4:8]
    pools = [scratch[8:9], scratch[9:10], scratch[10:11], scratch[11:13]]
    first, bias_v = scratch[13:15]
    xs_send, xs_recv, pt_send, pt_recv, bd_send, bd_recv, ld_sem, near, go, codes, sends = scratch[15:]

    dom = lax.axis_index("dom")
    me = lax.axis_index("batch")
    chip, core = me // CORES, me % CORES
    right = lax.rem(chip + 1, CHIPS) * CORES + core
    left = lax.rem(chip + CHIPS - 1, CHIPS) * CORES + core
    far = lax.rem(chip + 2, CHIPS) * CORES + core
    partner = chip * CORES + 1 - core
    offsets = (1, 2, parts - 1, parts // 2)

    barrier = pltpu.get_barrier_semaphore()

    def tell(semaphore, **peer):
        pl.semaphore_signal(semaphore, inc=1, device_id=peer, device_id_type=MESH)

    @pl.when(core == 0)
    def _():
        for peer in (left, right):
            tell(barrier, batch=peer)

    @pl.when(core == 1)
    def _():
        tell(barrier, batch=partner)

    loads = []

    def load(source, target):
        copy = pltpu.make_async_copy(source, target, ld_sem.at[len(loads)])
        copy.start()
        loads.append(copy)

    load(weights.at[0], wbufs[0].at[me])
    load(codes_in, codes)
    load(sends_in, sends)
    for j in range(BLK):
        load(act.at[:, pl.ds(j * TILE, TILE)], first.at[j])

    def piece(l, direction, slot, b):
        begin = (direction if slot != 1 else 1 - direction) * HALF
        count = HALF
        if slot > 1:
            count = HALF // SUBS
            begin = begin + (slot - 2) * count
        return wbufs[l].at[b, pl.ds(begin, count)]

    def ring(l, direction, slot, b):
        ref = piece(l, direction, slot, b)
        return pltpu.make_async_remote_copy(
            src_ref=ref, dst_ref=ref,
            send_sem=xs_send.at[l, direction, slot], recv_sem=xs_recv.at[l, direction, slot],
            device_id={"batch": right if direction == 0 else left}, device_id_type=MESH)

    def origin(direction, slot):
        return (left, right)[direction] if slot < 2 else far

    def hand(l, slot, ref):
        return pltpu.make_async_remote_copy(
            src_ref=ref, dst_ref=ref, send_sem=pt_send.at[l, slot], recv_sem=pt_recv.at[l, slot],
            device_id={"batch": partner}, device_id_type=MESH)

    def hand_wait(l):
        for slot in range(SLOTS):
            for direction in range(2):
                b = origin(direction, slot) + 1 - 2 * core
                hand(l, 2 * slot + direction, piece(l, direction, slot, b)).wait_recv()
        hand(l, 2 * SLOTS, wbufs[l].at[partner]).wait_recv()

    def hand_own(l):
        return hand(l, 2 * SLOTS, wbufs[l].at[me])

    def boundary(l, i, part):
        count = rows // len(pools[l])
        return pltpu.make_async_remote_copy(
            src_ref=stages[l].at[i, pl.ds(part * count, count)], dst_ref=pools[l][part].at[BLK + i],
            send_sem=bd_send.at[l, i, part], recv_sem=bd_recv.at[l, i, part],
            device_id={"dom": lax.rem(dom + offsets[i], parts)}, device_id_type=MESH)

    def boundary_start(l, part):
        @pl.when(last)
        def _():
            for i in (0, 1, 3, 2):
                boundary(l, i, part).start()

        @pl.when(jnp.logical_not(last))
        def _():
            for i in (3, 0, 1, 2):
                boundary(l, i, part).start()

    def boundary_wait(l, part):
        for i in range(NEIGH):
            boundary(l, i, part).wait_recv()

    def ring_own(l):
        for slot in range(2):
            for direction in range(2):
                ring(l, direction, slot, me).start()

    def step(l, s):
        for slot in (range(2, SLOTS) if s == 2 else (s,)):
            for direction in range(2):
                ring(l, direction, slot, origin(direction, slot)).wait_recv()
            if s == 0:
                for onward in range(2, SLOTS):
                    for direction in range(2):
                        ring(l, direction, onward, origin(direction, slot)).start()
                if l + 1 < LAYERS:
                    ring_own(l + 1)
            for direction in range(2):
                b = origin(direction, slot)
                hand(l, 2 * slot + direction, piece(l, direction, slot, b)).start()

    def block(l, j, part, start, count):
        pool = pools[l][part]
        x = jnp.concatenate([pool[codes[l, k, j], pl.ds(start, count)] for k in range(FAN)], axis=1)
        w = jnp.concatenate([wbufs[l][b, j] for b in range(SHARDS)], axis=0)
        summed = jnp.dot(x, w, preferred_element_type=jnp.float32)
        return jnp.maximum(summed + bias_v[j][l:l + 1], 0.0).astype(jnp.bfloat16)

    def sent(l):
        for slot in range(SLOTS):
            for direction in range(2):
                ring(l, direction, slot, me if slot < 2 else (left, right)[direction]).wait_send()
                hand(l, 2 * slot + direction, piece(l, direction, slot, origin(direction, slot))).wait_send()
        hand_own(l).wait_send()
        for part in range(len(pools[l])):
            for i in range(NEIGH):
                boundary(l, i, part).wait_send()

    loads[0].wait()

    @pl.when(core == 0)
    def _():
        pl.semaphore_wait(barrier, 3)
        for peer in (left, right):
            tell(near, batch=peer)
        ring_own(0)
        hand_own(0).start()
        pl.semaphore_wait(near, 2)
        tell(go, batch=partner)

    @pl.when(core == 1)
    def _():
        pl.semaphore_wait(go, 1)
        for offset in offsets:
            tell(barrier, dom=lax.rem(dom + parts - offset, parts))
        ring_own(0)
        hand_own(0).start()

    for copy in loads[1:]:
        copy.wait()
    done = len(loads)
    for l in range(1, LAYERS):
        load(weights.at[l], wbufs[l].at[me])
    for j in range(BLK):
        load(biases.at[:, pl.ds(j * TILE, TILE)], bias_v.at[j])
    for j in range(BLK):
        load(act.at[:, pl.ds(j * TILE, TILE)], pools[0][0].at[j])
    for i in (3, 0, 1, 2):
        stages[0][i] = first[sends[0, 0, i]]
    for copy in loads[done:]:
        copy.wait()

    soon = dom < parts // 4
    last = dom >= parts - 4

    @pl.when(soon)
    def _():
        step(0, 0)

    @pl.when(core == 1)
    def _():
        pl.semaphore_wait(barrier, NEIGH)
        tell(go, batch=partner)

    @pl.when(core == 0)
    def _():
        pl.semaphore_wait(go, 1)

    boundary_start(0, 0)
    for l in range(1, LAYERS):
        hand_own(l).start()

    @pl.when(jnp.logical_not(soon))
    def _():
        step(0, 0)

    for l in range(LAYERS):
        step(l, 1)
        step(l, 2)
        if l + 1 < LAYERS:
            @pl.when(soon)
            def _():
                step(l + 1, 0)
        hand_wait(l)
        if l + 1 < LAYERS:
            boundary_wait(l, 0)
            count = rows // len(pools[l + 1])
            for part in range(len(pools[l + 1])):
                early = [block(l, sends[l + 1, 0, i], 0, part * count, count) for i in range(NEIGH)]
                for i in range(NEIGH):
                    stages[l + 1][i, pl.ds(part * count, count)] = early[i]
                boundary_start(l + 1, part)

            @pl.when(jnp.logical_not(soon))
            def _():
                step(l + 1, 0)

            @pl.loop(0, BLK // GROUP)
            def _(g):
                js = [g * GROUP + u for u in range(GROUP)]
                values = [block(l, j, 0, 0, rows) for j in js]
                for j, value in zip(js, values):
                    for part in range(len(pools[l + 1])):
                        pools[l + 1][part][j] = value[part * count:(part + 1) * count]
        else:
            count = rows // len(pools[l])
            for layer in range(LAYERS - 1):
                sent(layer)
            for part in range(len(pools[l])):
                boundary_wait(l, part)

                @pl.loop(0, BLK // LAST_GROUP)
                def _(g):
                    js = [g * LAST_GROUP + u for u in range(LAST_GROUP)]
                    values = [block(l, j, part, 0, count) for j in js]
                    for j, value in zip(js, values):
                        columns = pl.ds(pl.multiple_of(j * TILE, TILE), TILE)
                        out[pl.ds(part * count, count), columns] = value
    sent(LAYERS - 1)


def body(activations, tile_weights, biases, source_codes, send_list):
    rows = activations.shape[0]
    parts = lax.axis_size("dom")
    part_rows = FAN * TILE // SHARDS
    anywhere = pl.BlockSpec(memory_space=pl.ANY)
    dma = pltpu.SemaphoreType.DMA
    return pl.pallas_call(
        lambda *refs: kernel(parts, rows, *refs),
        out_shape=pltpu.VMEM((rows, BLK * TILE), jnp.bfloat16),
        in_specs=[anywhere] * 5,
        out_specs=pl.BlockSpec(memory_space=pltpu.VMEM),
        scratch_shapes=(
            [pltpu.VMEM((SHARDS, BLK, part_rows, TILE), jnp.bfloat16)] * LAYERS
            + [pltpu.VMEM((NEIGH, rows, TILE), jnp.bfloat16)] * LAYERS
            + [pltpu.VMEM((BLK + NEIGH, rows, TILE), jnp.bfloat16)] * (LAYERS - 1)
            + [pltpu.VMEM((BLK + NEIGH, rows // 2, TILE), jnp.bfloat16)] * 2
            + [
                pltpu.VMEM((BLK, rows, TILE), jnp.bfloat16),
                pltpu.VMEM((BLK, LAYERS, TILE), jnp.float32),
                dma((LAYERS, 2, SLOTS)), dma((LAYERS, 2, SLOTS)),
                dma((LAYERS, 2 * SLOTS + 1)), dma((LAYERS, 2 * SLOTS + 1)),
                dma((LAYERS, NEIGH, 2)), dma((LAYERS, NEIGH, 2)),
                dma((3 * BLK + LAYERS + 2,)),
                pltpu.SemaphoreType.REGULAR, pltpu.SemaphoreType.REGULAR,
                pltpu.SMEM(source_codes.shape[:1] + source_codes.shape[:0:-1], jnp.int32), pltpu.SMEM(send_list.shape, jnp.int32),
            ]
        ),
        compiler_params=pltpu.CompilerParams(collective_id=0, has_side_effects=True),
        name="layers",
    )(activations, tile_weights, biases, jnp.transpose(source_codes, (0, 2, 1)), send_list)


def solution(mesh):
    in_specs = (
        P("batch", "dom"),
        P(None, "dom", "batch", None),
        P(None, "dom"),
        P(None, "dom", None),
        P(None, "dom", None),
    )
    out_specs = P("batch", "dom")
    return jax.shard_map(body, mesh=mesh, in_specs=in_specs, out_specs=out_specs, check_vma=False)
```

```python
import jax
import jax.numpy as jnp
from jax import lax
from jax.experimental import pallas as pl
from jax.experimental.pallas import tpu as pltpu
from jax.sharding import PartitionSpec as P

MESH = pl.DeviceIdType.MESH
LAYERS, BLK, FAN, TILE, NEIGH = 4, 16, 4, 128, 4
CHIPS, CORES = 4, 2
SHARDS = CHIPS * CORES
HALF = BLK // 2
SUBS = 2
SLOTS = 2 + SUBS
GROUP = 4
LAST_GROUP = 16


def kernel(parts, rows, act, weights, biases, codes_in, sends_in, out, *scratch):
    wbufs, stages = scratch[0:4], scratch[4:8]
    pools = [scratch[8:9], scratch[9:10], scratch[10:11], scratch[11:13]]
    first, bias_v = scratch[13:15]
    xs_send, xs_recv, pt_send, pt_recv, bd_send, bd_recv, ld_sem, near, go, codes, sends = scratch[15:]

    dom = lax.axis_index("dom")
    me = lax.axis_index("batch")
    chip, core = me // CORES, me % CORES
    right = lax.rem(chip + 1, CHIPS) * CORES + core
    left = lax.rem(chip + CHIPS - 1, CHIPS) * CORES + core
    far = lax.rem(chip + 2, CHIPS) * CORES + core
    partner = chip * CORES + 1 - core
    offsets = (1, 2, parts - 1, parts // 2)

    barrier = pltpu.get_barrier_semaphore()

    def tell(semaphore, **peer):
        pl.semaphore_signal(semaphore, inc=1, device_id=peer, device_id_type=MESH)

    @pl.when(core == 0)
    def _():
        for peer in (left, right):
            tell(barrier, batch=peer)

    @pl.when(core == 1)
    def _():
        tell(barrier, batch=partner)

    loads = []

    def load(source, target):
        copy = pltpu.make_async_copy(source, target, ld_sem.at[len(loads)])
        copy.start()
        loads.append(copy)

    load(weights.at[0], wbufs[0].at[me])
    load(codes_in, codes)
    load(sends_in, sends)
    for j in range(BLK):
        load(act.at[:, pl.ds(j * TILE, TILE)], first.at[j])

    def piece(l, direction, slot, b):
        begin = (direction if slot != 1 else 1 - direction) * HALF
        count = HALF
        if slot > 1:
            count = HALF // SUBS
            begin = begin + (slot - 2) * count
        return wbufs[l].at[b, pl.ds(begin, count)]

    def ring(l, direction, slot, b):
        ref = piece(l, direction, slot, b)
        return pltpu.make_async_remote_copy(
            src_ref=ref, dst_ref=ref,
            send_sem=xs_send.at[l, direction, slot], recv_sem=xs_recv.at[l, direction, slot],
            device_id={"batch": right if direction == 0 else left}, device_id_type=MESH)

    def origin(direction, slot):
        return (left, right)[direction] if slot < 2 else far

    def hand(l, slot, ref):
        return pltpu.make_async_remote_copy(
            src_ref=ref, dst_ref=ref, send_sem=pt_send.at[l, slot], recv_sem=pt_recv.at[l, slot],
            device_id={"batch": partner}, device_id_type=MESH)

    def hand_wait(l):
        for slot in range(SLOTS):
            for direction in range(2):
                b = origin(direction, slot) + 1 - 2 * core
                hand(l, 2 * slot + direction, piece(l, direction, slot, b)).wait_recv()
        hand(l, 2 * SLOTS, wbufs[l].at[partner]).wait_recv()

    def hand_own(l):
        return hand(l, 2 * SLOTS, wbufs[l].at[me])

    def boundary(l, i, part):
        count = rows // len(pools[l])
        return pltpu.make_async_remote_copy(
            src_ref=stages[l].at[i, pl.ds(part * count, count)], dst_ref=pools[l][part].at[BLK + i],
            send_sem=bd_send.at[l, i, part], recv_sem=bd_recv.at[l, i, part],
            device_id={"dom": lax.rem(dom + offsets[i], parts)}, device_id_type=MESH)

    def boundary_start(l, part):
        @pl.when(last)
        def _():
            for i in (1, 0, 3, 2):
                boundary(l, i, part).start()

        @pl.when(jnp.logical_not(last))
        def _():
            for i in ((3, 0, 1, 2) if part == 0 else (1, 0, 3, 2)):
                boundary(l, i, part).start()

    def boundary_wait(l, part):
        for i in range(NEIGH):
            boundary(l, i, part).wait_recv()

    def ring_own(l):
        for slot in range(2):
            for direction in range(2):
                ring(l, direction, slot, me).start()

    def step(l, s):
        for slot in (range(2, SLOTS) if s == 2 else (s,)):
            for direction in range(2):
                ring(l, direction, slot, origin(direction, slot)).wait_recv()
            if s == 0:
                for onward in range(2, SLOTS):
                    for direction in range(2):
                        ring(l, direction, onward, origin(direction, slot)).start()
                if l + 1 < LAYERS:
                    ring_own(l + 1)
            for direction in range(2):
                b = origin(direction, slot)
                hand(l, 2 * slot + direction, piece(l, direction, slot, b)).start()

    def block(l, j, part, start, count):
        pool = pools[l][part]
        x = jnp.concatenate([pool[codes[l, k, j], pl.ds(start, count)] for k in range(FAN)], axis=1)
        w = jnp.concatenate([wbufs[l][b, j] for b in range(SHARDS)], axis=0)
        summed = jnp.dot(x, w, preferred_element_type=jnp.float32)
        return jnp.maximum(summed + bias_v[j][l:l + 1], 0.0).astype(jnp.bfloat16)

    def sent(l):
        for slot in range(SLOTS):
            for direction in range(2):
                ring(l, direction, slot, me if slot < 2 else (left, right)[direction]).wait_send()
                hand(l, 2 * slot + direction, piece(l, direction, slot, origin(direction, slot))).wait_send()
        hand_own(l).wait_send()
        for part in range(len(pools[l])):
            for i in range(NEIGH):
                boundary(l, i, part).wait_send()

    loads[0].wait()

    @pl.when(core == 0)
    def _():
        pl.semaphore_wait(barrier, 3)
        for peer in (left, right):
            tell(near, batch=peer)
        ring_own(0)
        pl.semaphore_wait(near, 2)
        tell(go, batch=partner)
        hand_own(0).start()

    @pl.when(core == 1)
    def _():
        pl.semaphore_wait(go, 1)
        ring_own(0)
        for offset in offsets:
            tell(barrier, dom=lax.rem(dom + parts - offset, parts))
        hand_own(0).start()

    for copy in loads[1:]:
        copy.wait()
    done = len(loads)
    for l in range(1, LAYERS):
        load(weights.at[l], wbufs[l].at[me])
    for j in range(BLK):
        load(biases.at[:, pl.ds(j * TILE, TILE)], bias_v.at[j])
    for j in range(BLK):
        load(act.at[:, pl.ds(j * TILE, TILE)], pools[0][0].at[j])
    for i in (3, 0, 1, 2):
        stages[0][i] = first[sends[0, 0, i]]
    for copy in loads[done:]:
        copy.wait()

    soon = dom < parts // 4
    last = dom >= parts - 4

    @pl.when(soon)
    def _():
        step(0, 0)

    @pl.when(core == 1)
    def _():
        pl.semaphore_wait(barrier, NEIGH)
        tell(go, batch=partner)

    @pl.when(core == 0)
    def _():
        pl.semaphore_wait(go, 1)

    boundary_start(0, 0)
    for l in range(1, LAYERS):
        hand_own(l).start()

    @pl.when(jnp.logical_not(soon))
    def _():
        step(0, 0)

    for l in range(LAYERS):
        step(l, 1)
        step(l, 2)
        if l + 1 < LAYERS:
            @pl.when(soon)
            def _():
                step(l + 1, 0)
        hand_wait(l)
        if l + 1 < LAYERS:
            boundary_wait(l, 0)
            count = rows // len(pools[l + 1])
            for part in range(len(pools[l + 1])):
                early = [block(l, sends[l + 1, 0, i], 0, part * count, count) for i in range(NEIGH)]
                for i in range(NEIGH):
                    stages[l + 1][i, pl.ds(part * count, count)] = early[i]
                boundary_start(l + 1, part)

            @pl.when(jnp.logical_not(soon))
            def _():
                step(l + 1, 0)

            @pl.loop(0, BLK // GROUP)
            def _(g):
                js = [g * GROUP + u for u in range(GROUP)]
                values = [block(l, j, 0, 0, rows) for j in js]
                for j, value in zip(js, values):
                    for part in range(len(pools[l + 1])):
                        pools[l + 1][part][j] = value[part * count:(part + 1) * count]
        else:
            count = rows // len(pools[l])
            for layer in range(LAYERS - 1):
                sent(layer)
            for part in range(len(pools[l])):
                boundary_wait(l, part)

                @pl.loop(0, BLK // LAST_GROUP)
                def _(g):
                    js = [g * LAST_GROUP + u for u in range(LAST_GROUP)]
                    values = [block(l, j, part, 0, count) for j in js]
                    for j, value in zip(js, values):
                        columns = pl.ds(pl.multiple_of(j * TILE, TILE), TILE)
                        out[pl.ds(part * count, count), columns] = value
    sent(LAYERS - 1)


def body(activations, tile_weights, biases, source_codes, send_list):
    rows = activations.shape[0]
    parts = lax.axis_size("dom")
    part_rows = FAN * TILE // SHARDS
    anywhere = pl.BlockSpec(memory_space=pl.ANY)
    dma = pltpu.SemaphoreType.DMA
    return pl.pallas_call(
        lambda *refs: kernel(parts, rows, *refs),
        out_shape=pltpu.VMEM((rows, BLK * TILE), jnp.bfloat16),
        in_specs=[anywhere] * 5,
        out_specs=pl.BlockSpec(memory_space=pltpu.VMEM),
        scratch_shapes=(
            [pltpu.VMEM((SHARDS, BLK, part_rows, TILE), jnp.bfloat16)] * LAYERS
            + [pltpu.VMEM((NEIGH, rows, TILE), jnp.bfloat16)] * LAYERS
            + [pltpu.VMEM((BLK + NEIGH, rows, TILE), jnp.bfloat16)] * (LAYERS - 1)
            + [pltpu.VMEM((BLK + NEIGH, rows // 2, TILE), jnp.bfloat16)] * 2
            + [
                pltpu.VMEM((BLK, rows, TILE), jnp.bfloat16),
                pltpu.VMEM((BLK, LAYERS, TILE), jnp.float32),
                dma((LAYERS, 2, SLOTS)), dma((LAYERS, 2, SLOTS)),
                dma((LAYERS, 2 * SLOTS + 1)), dma((LAYERS, 2 * SLOTS + 1)),
                dma((LAYERS, NEIGH, 2)), dma((LAYERS, NEIGH, 2)),
                dma((3 * BLK + LAYERS + 2,)),
                pltpu.SemaphoreType.REGULAR, pltpu.SemaphoreType.REGULAR,
                pltpu.SMEM(source_codes.shape[:1] + source_codes.shape[:0:-1], jnp.int32), pltpu.SMEM(send_list.shape, jnp.int32),
            ]
        ),
        compiler_params=pltpu.CompilerParams(collective_id=0, has_side_effects=True),
        name="layers",
    )(activations, tile_weights, biases, jnp.transpose(source_codes, (0, 2, 1)), send_list)


def solution(mesh):
    in_specs = (
        P("batch", "dom"),
        P(None, "dom", "batch", None),
        P(None, "dom"),
        P(None, "dom", None),
        P(None, "dom", None),
    )
    out_specs = P("batch", "dom")
    return jax.shard_map(body, mesh=mesh, in_specs=in_specs, out_specs=out_specs, check_vma=False)
```
